128 devices in a mesh: row: 2 (over core), blk: 64 (over x, z, y).
Axes of the slice: x: 4, y: 4, z: 4, core: 2. Of those that a mesh axis runs over, the one named last changes fastest.
Arguments:
- flow_state: float32 [2, 64, 6, 16, 64, 256], P('row', 'blk'), may hold values from -6 to 6
- forcing: float32 [2, 64, 6, 16, 64, 256], P('row', 'blk'), may hold values from -6 to 6
- stiffness: float32 [2, 64, 16, 64, 256], P('row', 'blk'), may hold values from 7 to 14
- advection: float32 [2, 64, 6, 6], P('row', 'blk'), may hold values from -4 to 4
- line_inverse: float32 [2, 64, 96, 96], P('row', 'blk')
- margin_rows: int32 [2, 64, 64, 4], P('row', 'blk'), may hold values from 0 to 67, as said below
- margin_weights: float32 [2, 64, 64, 4], P('row', 'blk'), may hold values from 0 to 1, as said below
- partner_bit: int32 [2, 64], P('row', 'blk'), may hold values from 0 to 2, as said below
- turn_code: int32 [2, 64], P('row', 'blk'), may hold values from 0 to 3, as said below
Outputs:
- final_state: float32 [2, 64, 6, 16, 64, 256], P('row', 'blk')
The draws below stay inside these ranges and needn't reach their ends.
Inputs may be any that keep to these rules, and one draw needn't show every extreme that they name: Within a blade row, blocks 8g to 8g+7 share one value, so that b and b XOR 2**partner_bit[r,b] name each other. `turn_code`: A block and its face partner carry the same code. `margin_rows`: row j of a block reads window rows j to j + 4 only. `margin_weights`: the first 1 to 4 slots of a row carry positive weights summing to one, the others zero.
All inputs are finite; a program needn't handle non-finite values.
Results may differ from the reference program's by a relative error of at most 0.0001.
Values sent between devices are 32-bit elements; how exact they have to be, the bound alone decides.
No kernel may reach another device: no remote copies, remote signals or barrier semaphores. Data moves between devices by JAX's collectives and lax.ppermute only.
A program may use at most 128 MiB of HBM per device.

```python
import math
import jax
import jax.numpy as jnp
from jax import lax

NVAR = 6
NI = 16
NJ = 64
NK = 256
OV = 4
HW = 2
SWEEPS = 3
ROWS = 2
NBLK = 64


def pair_groups(key):
    picked = jax.random.randint(jax.random.fold_in(key, 11), (ROWS, NBLK // 8), 0, 3)
    picked = picked.at[0, 0].set(2).at[1, 0].set(0)
    return jnp.repeat(picked, 8, axis=1).astype(jnp.int32)


def margin_layout(key):
    counts = jax.random.randint(jax.random.fold_in(key, 17), (ROWS, NBLK, NJ), 1, OV + 1)
    offsets = jax.random.randint(jax.random.fold_in(key, 19), (ROWS, NBLK, NJ, OV), -HW, HW + 1)
    centre = jnp.arange(NJ, dtype=jnp.int32)[None, None, :, None] + HW
    chosen = centre + offsets
    chosen = chosen.at[:, :, NJ - 1, 0].set(NJ - 1 + 2 * HW).at[:, :, 0, 0].set(0)
    return (counts.astype(jnp.int32), chosen.astype(jnp.int32))


def draw_partner_bit(key, part):
    return pair_groups(key)


def draw_turn_code(key, part):
    levels = pair_groups(key)
    raw_codes = jax.random.randint(jax.random.fold_in(key, 13), (ROWS, NBLK), 0, 4)
    raw_codes = raw_codes.at[0, 0].set(3).at[1, 0].set(0)
    blocks = jnp.arange(NBLK, dtype=jnp.int32)[None, :]
    partner = jnp.bitwise_xor(blocks, jnp.left_shift(jnp.int32(1), levels))
    lowest = jnp.minimum(blocks, partner)
    return jnp.take_along_axis(raw_codes, lowest, axis=1).astype(jnp.int32)


def draw_margin_rows(key, part):
    counts, chosen = margin_layout(key)
    return chosen


def draw_margin_weights(key, part):
    counts, chosen = margin_layout(key)
    raw_weights = jax.random.uniform(jax.random.fold_in(key, 23), (ROWS, NBLK, NJ, OV), jnp.float32, 0.2, 1.0)
    active = jnp.arange(OV, dtype=jnp.int32)[None, None, None, :] < counts[..., None]
    kept = jnp.where(active, raw_weights, 0.0)
    return (kept / jnp.sum(kept, axis=-1, keepdims=True)).astype(jnp.float32)


def draw_line_inverse(key, part):
    order = NVAR * NI
    spread = 0.03 * jax.random.normal(key, (ROWS, NBLK, order, order), jnp.float32)
    identity = jnp.eye(order, dtype=jnp.float32)
    return (0.1 * (identity + spread)).astype(jnp.float32)


def steps_of(stream_key, dims, cuts, low, top_value):
    gain = 1.0
    for dim, shards_of in cuts:
        draws = jax.random.uniform(jax.random.fold_in(jax.random.fold_in(stream_key, 6), dim), (shards_of,), jnp.float32, low / len(cuts), top_value / len(cuts))
        gain = gain * jnp.repeat(jnp.exp(draws), dims[dim] // shards_of).reshape((-1,) + (1,) * (len(dims) - 1 - dim))
    return gain


def scatter_about(rng, dims, scale, reach, split=(), held_as=jnp.bfloat16):
    drawn = scale * jax.random.normal(rng, dims, jnp.float32)
    if split:
        drawn = drawn * steps_of(rng, dims, split, -0.22, 0.18)
    return jnp.clip(drawn, -reach, reach).astype(held_as)


def setup_inputs(seed: int = 0) -> dict:
    keys = jax.random.split(jax.random.key(seed), 10)
    return {
        "flow_state": scatter_about(keys[0], (ROWS, NBLK, NVAR, NI, NJ, NK), 1.0, 6.0, ((0, 2), (1, 64)), jnp.float32),
        "forcing": scatter_about(keys[1], (ROWS, NBLK, NVAR, NI, NJ, NK), 1.0, 6.0, ((0, 2), (1, 64)), jnp.float32),
        "stiffness": jnp.clip(jnp.exp(math.log(14.0) - 0.6931472 * jax.random.uniform(keys[2], (ROWS, NBLK, NI, NJ, NK), jnp.float32) ** steps_of(keys[2], (ROWS, NBLK, NI, NJ, NK), ((0, 2), (1, 64)), -0.2, 0.2)), 7.0, 14.0),
        "advection": scatter_about(keys[3], (ROWS, NBLK, NVAR, NVAR), 0.8, 4.0, ((0, 2), (1, 64)), jnp.float32),
        "line_inverse": draw_line_inverse(jax.random.fold_in(keys[9], 71), 0),
        "margin_rows": draw_margin_rows(jax.random.fold_in(keys[9], 71), 0),
        "margin_weights": draw_margin_weights(jax.random.fold_in(keys[9], 71), 0),
        "partner_bit": draw_partner_bit(jax.random.fold_in(keys[9], 71), 0),
        "turn_code": draw_turn_code(jax.random.fold_in(keys[9], 71), 0),
    }


def orient(surface, turn_code):
    flipped = jnp.flip(surface, -2)
    first = jnp.where((turn_code % 2 == 1)[..., None, None, None], flipped, surface)
    second = jnp.flip(first, -1)
    return jnp.where((turn_code // 2 == 1)[..., None, None, None], second, first)


def blend_matrix(rows_used, weights, extent):
    onehot = (rows_used[..., None] == jnp.arange(extent, dtype=jnp.int32)).astype(jnp.float32)
    return jnp.sum(weights[..., None] * onehot, axis=-2)


def operate(field, forcing, stiffness, advection, inlet_ghost, outlet_ghost, lower_ghost, upper_ghost):
    along_i = jnp.concatenate([inlet_ghost[..., None, :, :], field, outlet_ghost[..., None, :, :]], axis=-3)
    along_j = jnp.concatenate([lower_ghost[..., :, None, :], field, upper_ghost[..., :, None, :]], axis=-2)
    walls = jnp.zeros_like(field[..., :1])
    along_k = jnp.concatenate([walls, field, walls], axis=-1)
    neighbours = along_i[..., 2:, :, :] + along_i[..., :-2, :, :]
    neighbours = neighbours + along_j[..., 2:, :] + along_j[..., :-2, :]
    neighbours = neighbours + along_k[..., 2:] + along_k[..., :-2]
    stretch = along_i[..., 2:, :, :] - along_i[..., :-2, :, :]
    carried = 0.5 * jnp.einsum('...vw,...wijk->...vijk', advection, stretch, precision=lax.Precision.HIGHEST)
    return forcing - (stiffness[..., None, :, :, :] * field - neighbours + carried)


def reference(flow_state, forcing, stiffness, advection, line_inverse, margin_rows, margin_weights, partner_bit, turn_code):
    field = flow_state
    blend = blend_matrix(margin_rows, margin_weights, NJ + 2 * HW)
    row_index = jnp.arange(ROWS, dtype=jnp.int32)[:, None]
    partner = jnp.bitwise_xor(jnp.arange(NBLK, dtype=jnp.int32)[None, :], jnp.left_shift(jnp.int32(1), partner_bit))
    for sweep in range(SWEEPS):
        plane = jnp.stack([field[0, :, :, NI - 1], field[1, :, :, 0]])
        opposite = plane[::-1]
        before = jnp.roll(opposite, 1, axis=1)
        beyond = jnp.roll(opposite, -1, axis=1)
        window = jnp.concatenate([before[..., NJ - HW:, :], opposite, beyond[..., :HW, :]], axis=-2)
        ghosts = jnp.einsum('rbjm,rbvmk->rbvjk', blend, window, precision=lax.Precision.HIGHEST)
        inlet_ghost = jnp.stack([field[0, :, :, 0], ghosts[1]])
        outlet_ghost = jnp.stack([ghosts[0], field[1, :, :, NI - 1]])
        lower_face = field[:, :, :, :, 0, :]
        upper_face = field[:, :, :, :, NJ - 1, :]
        lower_ghost = orient(upper_face[row_index, partner], turn_code)
        upper_ghost = orient(lower_face[row_index, partner], turn_code)
        residue = operate(field, forcing, stiffness, advection, inlet_ghost, outlet_ghost, lower_ghost, upper_ghost)
        flat = residue.reshape((ROWS, NBLK, NVAR * NI, NJ * NK))
        change = jnp.einsum('rbmn,rbnl->rbml', line_inverse, flat, precision=lax.Precision.HIGHEST)
        field = field + change.reshape(field.shape)
    return field
```

```python
import jax
import jax.numpy as jnp
from jax import lax
from jax.experimental import pallas as pl
from jax.experimental.pallas import tpu as pltpu
from jax.sharding import PartitionSpec as P

SWEEPS = 3
NV, NI, NJ, NK = 6, 16, 64, 256
LN = NV * NI
F32, BF16 = jnp.float32, jnp.bfloat16
VM = pl.BlockSpec(memory_space=pltpu.VMEM)
SM = pl.BlockSpec(memory_space=pltpu.SMEM)
HI = lax.Precision.HIGHEST
BLOCK = 4


def params(mib):
    return pltpu.CompilerParams(vmem_limit_bytes=mib << 20)


def iota(shape, dim):
    return lax.broadcasted_iota(jnp.int32, shape, dim)


def hot(mask):
    return jnp.where(mask, 1.0, 0.0).astype(F32)


def high_part(x):
    return x.astype(BF16).astype(F32)


def dot_exact(a, b):
    return jnp.dot(a, b, precision=HI, preferred_element_type=F32)


def prepare_kernel(flags, inverse, jacobian, sweep_w, ghost_w, face_w, flip_w):
    rotor = flags[0] == 0
    code = flags[1]
    lines = inverse[...]
    r, c = iota((LN, LN), 0), iota((LN, LN), 1)
    rv, ri, cv, ci = r // NI, r % NI, c // NI, c % NI
    expand = hot(iota((LN, 8), 0) // NI == iota((LN, 8), 1))
    collect = hot(iota((8, LN), 1) // NI == iota((8, LN), 0))
    flux = dot_exact(dot_exact(expand, jacobian[...]), collect)
    last = NI - 1
    self_above = jnp.logical_and(ri == last, ci == last)
    self_below = jnp.logical_and(ri == 0, ci == 0)
    is_rotor = jnp.where(rotor, 1.0, 0.0)
    above = hot(ci == ri + 1) + hot(self_above) * (1.0 - is_rotor)
    below = hot(ri == ci + 1) + hot(self_below) * is_rotor
    along = hot(rv == cv) * (above + below) - 0.5 * flux * (above - below)
    both = dot_exact(lines, along)
    sign = jnp.where(rotor, 1.0, -1.0)
    edge = jnp.where(rotor, last, 0)
    g_row, g_col = iota((LN, 8), 0), iota((LN, 8), 1)
    spread = hot(g_row % NI == edge) * (
        hot(jnp.logical_and(g_row // NI == g_col, g_col < NV))
        - 0.5 * sign * dot_exact(expand, jacobian[...])
    )
    ghost = dot_exact(lines, spread)
    turned = dot_exact(lines, hot(jnp.logical_and(rv == cv, ri + ci == last)))
    face = jnp.where(code % 2 == 1, turned, lines)

    def place(rows, cols, starts):
        k, m = iota((rows, cols), 0), iota((rows, cols), 1)
        total = hot(m == k + starts[0])
        for start in starts[1:]:
            total = total + hot(m == k + start)
        return total

    def split(matrix):
        top = high_part(matrix)
        return top, high_part(matrix - top)

    l_hi, l_lo = split(lines)
    b_hi, b_lo = split(both)
    width = 4 * LN
    sweep_w[:LN] = (
        dot_exact(l_hi, place(LN, width, (0, LN)))
        + dot_exact(b_hi, place(LN, width, (2 * LN, 3 * LN)))
    ).astype(BF16)
    sweep_w[LN:] = (
        dot_exact(l_lo, place(LN, width, (0,))) + dot_exact(b_lo, place(LN, width, (2 * LN,)))
    ).astype(BF16)
    g_hi, g_lo = split(ghost)
    ghost_w[:LN] = dot_exact(g_hi, place(8, 16, (0, 8))).astype(BF16)
    ghost_w[LN:] = dot_exact(g_lo, place(8, 16, (0,))).astype(BF16)
    f_hi, f_lo = split(face)
    face_w[:LN] = dot_exact(f_hi, place(LN, 2 * LN, (0, LN))).astype(BF16)
    face_w[LN:] = dot_exact(f_lo, place(LN, 2 * LN, (0,))).astype(BF16)
    a, b = iota((NK, NK), 0), iota((NK, NK), 1)
    mirrored = hot(a + b == NK - 1)
    flip_w[...] = jnp.where(code // 2 == 1, mirrored, hot(a == b)).astype(BF16)


def prepare(flags, inverse, jacobian):
    return pl.pallas_call(
        prepare_kernel,
        out_shape=[
            pltpu.VMEM((2 * LN, 4 * LN), BF16),
            pltpu.VMEM((2 * LN, 16), BF16),
            pltpu.VMEM((2 * LN, 2 * LN), BF16),
            pltpu.VMEM((NK, NK), BF16),
        ],
        in_specs=[SM, VM, VM],
        out_specs=[VM] * 4,
        compiler_params=params(6),
        name="prepare",
    )(flags, inverse, jacobian)


def halves(x):
    top = x.astype(BF16)
    return top, (x - top.astype(F32)).astype(BF16)


def shifted(x):
    half = NK // 2
    a, b = x[:, :half], x[:, half:]
    lane = iota((8, half), 1)
    first = jnp.tile(lane == 0, (x.shape[0] // 8, 1))
    end = jnp.tile(lane == half - 1, (x.shape[0] // 8, 1))
    ra, rb = pltpu.roll(a, 1, 1), pltpu.roll(b, 1, 1)
    la, lb = pltpu.roll(a, half - 1, 1), pltpu.roll(b, half - 1, 1)
    zero = jnp.zeros_like(a)
    left = [jnp.where(first, zero, ra), jnp.where(first, ra, rb)]
    right = [jnp.where(end, lb, la), jnp.where(end, zero, lb)]
    return jnp.concatenate([left[0] + right[0], left[1] + right[1]], axis=1)


def interior_kernel(state, source, diagonal, weights, out, stack):
    def block(step, carry):
        base = step * BLOCK
        for n in range(BLOCK):
            j = base + n
            s = state[j]
            below = state[jnp.maximum(j - 1, 0)]
            above = state[jnp.minimum(j + 1, NJ - 1)]
            if n == 0:
                below = below * jnp.where(j == 0, 0.0, 1.0)
            if n == BLOCK - 1:
                above = above * jnp.where(j == NJ - 1, 0.0, 1.0)
            d = jnp.concatenate([diagonal[j]] * NV, axis=0)
            e = source[j] - d * s + (below + above) + shifted(s)
            e_hi, e_lo = halves(e)
            s_hi, s_lo = halves(s)
            cols = pl.ds(n * NK, NK)
            stack[0:LN, cols] = e_hi
            stack[LN : 2 * LN, cols] = e_lo
            stack[2 * LN : 3 * LN, cols] = s_hi
            stack[3 * LN :, cols] = s_lo
        for n in range(BLOCK):
            cols = pl.ds(n * NK, NK)
            both = jnp.dot(weights[...], stack[:, cols], preferred_element_type=F32)
            out[base + n] = state[base + n] + (both[:LN] + both[LN:])
        return carry

    lax.fori_loop(0, NJ // BLOCK, block, 0)


def interior(state, source, diagonal, weights):
    return pl.pallas_call(
        interior_kernel,
        out_shape=pltpu.VMEM((NJ, LN, NK), F32),
        in_specs=[VM] * 4,
        out_specs=VM,
        scratch_shapes=[pltpu.VMEM((4 * LN, BLOCK * NK), BF16)],
        compiler_params=params(4),
        cost_estimate=pl.CostEstimate(flops=4_800_000_000, bytes_accessed=14_000_000, transcendentals=0),
        name="interior",
    )(state, source, diagonal, weights)


def outer_kernel(coef, edge, part, plane, lo, hi, faces, ghost_w, face_w, flip_w, out, face_out, plane_out, window, stack):
    window[0:2] = lo[...]
    window[2 : NJ + 2] = plane[...]
    window[NJ + 2 :] = hi[...]
    rotor_side = edge[0] == 0

    def pick(x):
        rows = [jnp.where(rotor_side, x[v * NI + NI - 1 : v * NI + NI], x[v * NI : v * NI + 1]) for v in range(NV)]
        return jnp.concatenate(rows + [rows[-1], rows[-1]], axis=0)

    def ghost_of(j):
        total = coef[j, 0] * window[j]
        for d in range(1, 5):
            total = total + coef[j, d] * window[j + d]
        return total

    def block(step, carry):
        base = step * BLOCK
        for n in range(BLOCK):
            g_hi, g_lo = halves(ghost_of(base + n))
            g = jnp.concatenate([g_hi.astype(F32), g_lo.astype(F32)], axis=0).astype(BF16)
            both = jnp.dot(ghost_w[...], g, preferred_element_type=F32)
            out[base + n] = part[base + n] + (both[:LN] + both[LN:])
        return carry

    lax.fori_loop(0, NJ // BLOCK, block, 0)
    for side, j in ((1, 0), (0, NJ - 1)):
        f_hi, f_lo = halves(faces[side])
        stack[:LN] = f_hi
        stack[LN:] = f_lo
        turned = jnp.dot(stack[...], flip_w[...], preferred_element_type=F32).astype(BF16)
        both = jnp.dot(face_w[...], turned, preferred_element_type=F32)
        out[j] = out[j] + (both[:LN] + both[LN:])
    face_out[0] = out[0]
    face_out[1] = out[NJ - 1]

    def planes(step, carry):
        for n in range(BLOCK):
            plane_out[step * BLOCK + n] = pick(out[step * BLOCK + n])
        return carry

    lax.fori_loop(0, NJ // BLOCK, planes, 0)


def outer(coef, edge, part, plane, lo, hi, faces, ghost_w, face_w, flip_w):
    return pl.pallas_call(
        outer_kernel,
        out_shape=[
            pltpu.VMEM((NJ, LN, NK), F32),
            pltpu.VMEM((2, LN, NK), F32),
            pltpu.VMEM((NJ, 8, NK), F32),
        ],
        in_specs=[SM, SM] + [VM] * 8,
        out_specs=[VM] * 3,
        scratch_shapes=[pltpu.VMEM((NJ + 4, 8, NK), F32), pltpu.VMEM((2 * LN, NK), BF16)],
        input_output_aliases={2: 0},
        compiler_params=params(4),
        name="outer",
    )(coef, edge, part, plane, lo, hi, faces, ghost_w, face_w, flip_w)


def exchange(faces, plane, bit, blocks):
    def across(step):
        return [
            (r * blocks + b, (1 - r) * blocks + (b + step) % blocks)
            for r in range(2)
            for b in range(blocks)
        ]

    axes = ("row", "blk")
    lo = lax.ppermute(plane[NJ - 2 :], axes, across(1))
    hi = lax.ppermute(plane[:2], axes, across(-1))
    other = lax.ppermute(plane, "row", [(0, 1), (1, 0)])
    got = [lax.ppermute(faces, "blk", [(b, b ^ (1 << k)) for b in range(blocks)]) for k in range(3)]
    received = jnp.where(bit == 0, got[0], jnp.where(bit == 1, got[1], got[2]))
    return lo, hi, other, received


def body(flow_state, forcing, stiffness, advection, line_inverse, margin_rows, margin_weights, partner_bit, turn_code):
    blocks = lax.axis_size("blk")
    row = lax.axis_index("row")
    field = flow_state[0, 0]
    faces = jnp.stack([field[:, :, 0].reshape(LN, NK), field[:, :, NJ - 1].reshape(LN, NK)])
    plane = jnp.where(row == 0, field[:, NI - 1], field[:, 0])
    plane = jnp.pad(plane.transpose(1, 0, 2), ((0, 0), (0, 2), (0, 0)))
    comm = exchange(faces, plane, partner_bit[0, 0], blocks)
    state = field.reshape(LN, NJ, NK).transpose(1, 0, 2)
    source = forcing[0, 0].reshape(LN, NJ, NK).transpose(1, 0, 2)
    diagonal = stiffness[0, 0].transpose(1, 0, 2)
    slots = margin_rows[0, 0] - jnp.arange(NJ, dtype=jnp.int32)[:, None]
    coef = jnp.sum(
        jnp.where(slots[..., None] == jnp.arange(5, dtype=jnp.int32), margin_weights[0, 0][..., None], 0.0), axis=1
    )
    edge = row.reshape(1)
    flags = jnp.stack([row, turn_code[0, 0]])
    jac = jnp.pad(advection[0, 0], ((0, 2), (0, 2)))
    sweep_w, ghost_w, face_w, flip_w = prepare(flags, line_inverse[0, 0], jac)
    for sweep in range(SWEEPS):
        part = interior(state, source, diagonal, sweep_w)
        lo, hi, other, received = comm
        state, faces, plane = outer(coef, edge, part, other, lo, hi, received, ghost_w, face_w, flip_w)
        if sweep < SWEEPS - 1:
            comm = exchange(faces, plane, partner_bit[0, 0], blocks)
    return state.transpose(1, 0, 2).reshape(field.shape)[None, None]


def solution(mesh):
    return jax.shard_map(
        body,
        mesh=mesh,
        in_specs=(P("row", "blk"),) * 9,
        out_specs=P("row", "blk"),
        check_vma=False,
    )
```

```python
import functools

import jax
import jax.numpy as jnp
from jax import lax
from jax.experimental import pallas as pl
from jax.experimental.pallas import tpu as pltpu
from jax.sharding import PartitionSpec as P

SWEEPS = 3
NV, NI, NJ, NK = 6, 16, 64, 256
LN = NV * NI
F32, BF16 = jnp.float32, jnp.bfloat16
VM = pl.BlockSpec(memory_space=pltpu.VMEM)
SM = pl.BlockSpec(memory_space=pltpu.SMEM)
ANY = pl.BlockSpec(memory_space=pltpu.HBM)
HI = lax.Precision.HIGHEST
BLOCK = 8
STEPS = NJ // BLOCK


def params(mib):
    return pltpu.CompilerParams(vmem_limit_bytes=mib << 20)


def in_hbm(x):
    return pltpu.with_memory_space_constraint(x, pltpu.HBM)


def iota(shape, dim):
    return lax.broadcasted_iota(jnp.int32, shape, dim)


def hot(mask):
    return jnp.where(mask, 1.0, 0.0).astype(F32)


def high_part(x):
    return x.astype(BF16).astype(F32)


def dot_exact(a, b):
    return jnp.dot(a, b, precision=HI, preferred_element_type=F32)


def mul(a, b):
    return jnp.dot(a, b, preferred_element_type=F32)


def prepare_kernel(flags, inverse, jacobian, sweep_w, ghost_w, edge_w, face_w, flip_w):
    rotor = flags[0] == 0
    code = flags[1]
    lines = inverse[...]
    r, c = iota((LN, LN), 0), iota((LN, LN), 1)
    rv, ri, cv, ci = r // NI, r % NI, c // NI, c % NI
    expand = hot(iota((LN, 8), 0) // NI == iota((LN, 8), 1))
    collect = hot(iota((8, LN), 1) // NI == iota((8, LN), 0))
    flux = dot_exact(dot_exact(expand, jacobian[...]), collect)
    last = NI - 1
    self_above = jnp.logical_and(ri == last, ci == last)
    self_below = jnp.logical_and(ri == 0, ci == 0)
    is_rotor = jnp.where(rotor, 1.0, 0.0)
    above = hot(ci == ri + 1) + hot(self_above) * (1.0 - is_rotor)
    below = hot(ri == ci + 1) + hot(self_below) * is_rotor
    along = hot(rv == cv) * (above + below) - 0.5 * flux * (above - below)
    both = dot_exact(lines, along)
    sign = jnp.where(rotor, 1.0, -1.0)
    edge = jnp.where(rotor, last, 0)
    g_row, g_col = iota((LN, 8), 0), iota((LN, 8), 1)
    spread = hot(g_row % NI == edge) * (
        hot(jnp.logical_and(g_row // NI == g_col, g_col < NV))
        - 0.5 * sign * dot_exact(expand, jacobian[...])
    )
    ghost = dot_exact(lines, spread)
    turned = dot_exact(lines, hot(jnp.logical_and(rv == cv, ri + ci == last)))
    face = jnp.where(code % 2 == 1, turned, lines)

    def place(rows, cols, starts):
        k, m = iota((rows, cols), 0), iota((rows, cols), 1)
        total = hot(m == k + starts[0])
        for start in starts[1:]:
            total = total + hot(m == k + start)
        return total

    def split(matrix):
        top = high_part(matrix)
        return top, high_part(matrix - top)

    l_hi, l_lo = split(lines)
    b_hi, b_lo = split(both)
    width = 4 * LN
    sweep_w[:LN] = (
        dot_exact(l_hi, place(LN, width, (0, LN)))
        + dot_exact(b_hi, place(LN, width, (2 * LN, 3 * LN)))
    ).astype(BF16)
    sweep_w[LN:] = (
        dot_exact(l_lo, place(LN, width, (0,))) + dot_exact(b_lo, place(LN, width, (2 * LN,)))
    ).astype(BF16)
    g_hi, g_lo = split(ghost)
    full = dot_exact(g_hi, place(8, 32, (0, 8))) + dot_exact(g_lo, place(8, 32, (16,)))
    ghost_w[...] = full.astype(BF16)
    pick = hot(jnp.logical_and(iota((16, LN), 1) == NI * iota((16, LN), 0) + edge, iota((16, LN), 0) < NV))
    edge_w[...] = dot_exact(pick, full).astype(BF16)
    f_hi, f_lo = split(face)
    face_w[:LN] = dot_exact(f_hi, place(LN, 2 * LN, (0, LN))).astype(BF16)
    face_w[LN:] = dot_exact(f_lo, place(LN, 2 * LN, (0,))).astype(BF16)
    a, b = iota((NK, NK), 0), iota((NK, NK), 1)
    mirrored = hot(a + b == NK - 1)
    flip_w[...] = jnp.where(code // 2 == 1, mirrored, hot(a == b)).astype(BF16)


def prepare(flags, inverse, jacobian):
    return pl.pallas_call(
        prepare_kernel,
        out_shape=[
            pltpu.VMEM((2 * LN, 4 * LN), BF16),
            pltpu.VMEM((LN, 32), BF16),
            pltpu.VMEM((16, 32), BF16),
            pltpu.VMEM((2 * LN, 2 * LN), BF16),
            pltpu.VMEM((NK, NK), BF16),
        ],
        in_specs=[SM, VM, VM],
        out_specs=[VM] * 5,
        compiler_params=params(6),
        name="prepare",
    )(flags, inverse, jacobian)


HALF = NK // 2


def lanes(h):
    return pl.ds(h * HALF, HALF)


def begin_kernel(edge, state, face_out, plane_out, ends, cut, sems):
    at = edge[0]
    copies = []
    for h in range(2):
        copies.append(pltpu.make_async_copy(state.at[:, 0:8, lanes(h)], ends.at[0, h], sems.at[0, h]))
        copies.append(pltpu.make_async_copy(state.at[:, NJ - 8 : NJ, lanes(h)], ends.at[1, h], sems.at[1, h]))
        for v in range(NV):
            copies.append(pltpu.make_async_copy(state.at[v * NI + at, :, lanes(h)], cut.at[h, v], sems.at[2 + v, h]))
    for copy in copies:
        copy.start()
    for copy in copies:
        copy.wait()
    pad = jnp.zeros((2, HALF), F32)
    for h in range(2):
        for side in range(2):
            rows = ends.at[side, h].reshape(LN * 8, HALF)
            face_out[side, :, lanes(h)] = rows[pl.ds(7 * side, LN, stride=8), :]
        planes = cut.at[h].reshape(NV * NJ, HALF)
        for j in range(NJ):
            plane_out[j, :, lanes(h)] = jnp.concatenate([planes[pl.ds(j, NV, stride=NJ), :], pad], axis=0)


def begin(edge, state):
    return pl.pallas_call(
        begin_kernel,
        out_shape=[pltpu.VMEM((2, LN, NK), F32), pltpu.VMEM((NJ, 8, NK), F32)],
        in_specs=[SM, ANY],
        out_specs=[VM] * 2,
        scratch_shapes=[
            pltpu.VMEM((2, 2, LN, 8, HALF), F32),
            pltpu.VMEM((2, NV, NJ, HALF), F32),
            pltpu.SemaphoreType.DMA((2 + NV, 2)),
        ],
        compiler_params=params(4),
        name="begin",
    )(edge, state)


def halves(x):
    top = x.astype(BF16)
    return top, (x - top.astype(F32)).astype(BF16)


def shifted(x):
    half = NK // 2
    a, b = x[:, :half], x[:, half:]
    lane = iota(a.shape, 1)
    first, end = lane == 0, lane == half - 1
    ra, rb = pltpu.roll(a, 1, 1), pltpu.roll(b, 1, 1)
    la, lb = pltpu.roll(a, half - 1, 1), pltpu.roll(b, half - 1, 1)
    zero = jnp.zeros_like(a)
    left = jnp.where(first, zero, ra) + jnp.where(end, lb, la)
    right = jnp.where(first, ra, rb) + jnp.where(end, zero, lb)
    return jnp.concatenate([left, right], axis=1)


def fetches(pairs, sems):
    def copies(step, slot):
        rows = pl.ds(step * BLOCK, BLOCK)
        return [
            pltpu.make_async_copy(array.at[:, rows, lanes(h)], place(step, slot, h), sems.at[n, h, slot])
            for n, (array, place) in enumerate(pairs)
            for h in range(2)
        ]

    def start(step, slot):
        for copy in copies(step, slot):
            copy.start()

    def wait(step, slot):
        for copy in copies(step, slot):
            copy.wait()

    return start, wait


def joined(ref, at, count, stride, v):
    parts = []
    for h in range(2):
        half = ref.at[h].reshape(ref.shape[1] * ref.shape[2], HALF)
        parts.append(half[pl.ds(at + v * count * stride, count, stride=stride), :])
    return jnp.concatenate(parts, axis=1)


def relax(row, s_buf, d_buf, weights, out, stack):
    def gather(step, slot):
        for n in range(BLOCK):
            d = joined(d_buf.at[slot], n, NI, BLOCK, 0)
            for v in range(NV):
                s = row(step, n, v)
                if n == 0:
                    below = row(jnp.maximum(step - 1, 0), BLOCK - 1, v) * jnp.where(step == 0, 0.0, 1.0)
                else:
                    below = row(step, n - 1, v)
                if n == BLOCK - 1:
                    above = row(jnp.minimum(step + 1, STEPS - 1), 0, v) * jnp.where(step == STEPS - 1, 0.0, 1.0)
                else:
                    above = row(step, n + 1, v)
                e = joined(s_buf.at[slot], n, NI, BLOCK, v) - d * s + (below + above) + shifted(s)
                e_hi, e_lo = halves(e)
                s_hi, s_lo = halves(s)
                for k, part in enumerate((e_hi, e_lo, s_hi, s_lo)):
                    stack[slot, n, k * LN + v * NI : k * LN + (v + 1) * NI] = part

    def solve(step, slot):
        for n in range(BLOCK):
            both = mul(weights[...], stack[slot, n])
            for v in range(NV):
                at = v * NI
                change = both[at : at + NI] + both[LN + at : LN + at + NI]
                out[step * BLOCK + n, at : at + NI] = row(step, n, v) + change

    return gather, solve


def blend_ghosts(coef, window, j):
    total = coef[j, 0] * window[j]
    for d in range(1, 5):
        total = total + coef[j, d] * window[j + d]
    g_hi = high_part(total)
    g_lo = high_part(total - g_hi)
    return jnp.concatenate([g_hi, g_lo, g_hi, jnp.zeros_like(g_hi)], axis=0).astype(BF16)


def fill_window(window, lo, hi, plane):
    window[0:2] = lo[...]
    window[2 : NJ + 2] = plane[...]
    window[NJ + 2 :] = hi[...]


def turned_face(face, stack, face_w, flip_w):
    f_hi, f_lo = halves(face[...])
    stack[:LN] = f_hi
    stack[LN:] = f_lo
    both = mul(face_w[...], mul(stack[...], flip_w[...]).astype(BF16))
    return both[:LN] + both[LN:]


def interior_kernel(state, source, diagonal, weights, out, stack, s_buf, d_buf, sems, held, more):
    start, wait = fetches(
        [
            (source, lambda step, slot, h: s_buf.at[slot, h]),
            (diagonal, lambda step, slot, h: d_buf.at[slot, h]),
        ],
        sems,
    )

    def load(step):
        rows = pl.ds(step * BLOCK, BLOCK)
        return [
            pltpu.make_async_copy(state.at[:, rows, lanes(h)], held.at[step, h], more.at[h, step])
            for h in range(2)
        ]

    def arrived(step):
        for copy in load(step):
            copy.wait()

    def row(step, n, v):
        return joined(held.at[step], n, NI, BLOCK, v)

    gather, solve = relax(row, s_buf, d_buf, weights, out, stack)
    for step in range(STEPS):
        for copy in load(step):
            copy.start()
        if step < 2:
            start(step, step)
    arrived(0)
    arrived(1)
    wait(0, 0)
    gather(0, 0)
    wait(1, 1)

    def pair(step, carry):
        first = 2 * step

        @pl.when(first + 2 < STEPS)
        def _():
            start(first + 2, 0)
            arrived(first + 2)

        gather(first + 1, 1)
        solve(first, 0)

        @pl.when(first + 2 < STEPS)
        def _():
            start(first + 3, 1)
            arrived(first + 3)
            wait(first + 2, 0)

        gather(jnp.minimum(first + 2, STEPS - 1), 0)
        solve(first + 1, 1)

        @pl.when(first + 2 < STEPS)
        def _():
            wait(first + 3, 1)

        return carry

    lax.fori_loop(0, STEPS // 2, pair, 0)


RELAX_SCRATCH = [
    pltpu.VMEM((2, BLOCK, 4 * LN, NK), BF16),
    pltpu.VMEM((2, 2, LN, BLOCK, HALF), F32),
    pltpu.VMEM((2, 2, NI, BLOCK, HALF), F32),
    pltpu.SemaphoreType.DMA((2, 2, 2)),
]
RELAX_COST = pl.CostEstimate(flops=4_800_000_000, bytes_accessed=14_000_000, transcendentals=0)


def interior(state, source, diagonal, weights):
    return pl.pallas_call(
        interior_kernel,
        out_shape=pltpu.VMEM((NJ, LN, NK), F32),
        in_specs=[ANY, ANY, ANY, VM],
        out_specs=VM,
        scratch_shapes=RELAX_SCRATCH
        + [pltpu.VMEM((STEPS, 2, LN, BLOCK, HALF), F32), pltpu.SemaphoreType.DMA((2, STEPS))],
        compiler_params=params(16),
        cost_estimate=RELAX_COST,
        name="interior",
    )(state, source, diagonal, weights)


def advance_kernel(part, ghosts, faces, source, diagonal, weights, ghost_w, out, stack, s_buf, d_buf, sems, fresh):
    start, wait = fetches(
        [
            (source, lambda step, slot, h: s_buf.at[slot, h]),
            (diagonal, lambda step, slot, h: d_buf.at[slot, h]),
        ],
        sems,
    )

    def fix(step):
        for n in range(BLOCK):
            j = step * BLOCK + n
            value = part[j] + mul(ghost_w[...], ghosts[j])
            if n == BLOCK - 1:
                value = jnp.where(j == NJ - 1, faces[1], value)
            fresh[j] = value

    def row(step, n, v):
        return fresh[step * BLOCK + n, v * NI : (v + 1) * NI]

    gather, solve = relax(row, s_buf, d_buf, weights, out, stack)
    start(0, 0)
    start(1, 1)
    for step in range(3):
        fix(step)
    fresh[0] = faces[0]
    wait(0, 0)
    gather(0, 0)
    wait(1, 1)

    def pair(step, carry):
        first = 2 * step

        @pl.when(first + 2 < STEPS)
        def _():
            start(first + 2, 0)

        fix(jnp.minimum(first + 3, STEPS - 1))
        gather(first + 1, 1)
        solve(first, 0)

        @pl.when(first + 2 < STEPS)
        def _():
            start(first + 3, 1)
            wait(first + 2, 0)

        fix(jnp.minimum(first + 4, STEPS - 1))
        gather(jnp.minimum(first + 2, STEPS - 1), 0)
        solve(first + 1, 1)

        @pl.when(first + 2 < STEPS)
        def _():
            wait(first + 3, 1)

        return carry

    lax.fori_loop(0, STEPS // 2, pair, 0)


def advance(part, ghosts, faces, source, diagonal, weights, ghost_w):
    return pl.pallas_call(
        advance_kernel,
        out_shape=pltpu.VMEM((NJ, LN, NK), F32),
        in_specs=[VM, VM, VM, ANY, ANY, VM, VM],
        out_specs=VM,
        scratch_shapes=RELAX_SCRATCH + [pltpu.VMEM((NJ, LN, NK), F32)],
        compiler_params=params(16),
        cost_estimate=RELAX_COST,
        name="advance",
    )(part, ghosts, faces, source, diagonal, weights, ghost_w)


def border_kernel(
    coef, edge, part, plane, lo, hi, faces, ghost_w, edge_w, face_w, flip_w,
    ghosts, face_out, plane_out, window, stack,
):
    fill_window(window, lo, hi, plane)
    at = edge[0]

    def block(step, carry):
        for n in range(BLOCK):
            j = step * BLOCK + n
            g = blend_ghosts(coef, window, j)
            ghosts[j] = g
            rows = [part[j, pl.ds(v * NI + at, 1), :] for v in range(NV)]
            old = jnp.concatenate(rows + [jnp.zeros((2, NK), F32)], axis=0)
            plane_out[j] = old + mul(edge_w[...], g)[:8]
        return carry

    lax.fori_loop(0, STEPS, block, 0)
    for side, j in ((0, 0), (1, NJ - 1)):
        change = turned_face(faces.at[1 - side], stack, face_w, flip_w)
        face_out[side] = part[j] + mul(ghost_w[...], ghosts[j]) + change
        rows = [face_out[side, pl.ds(v * NI + at, 1), :] for v in range(NV)]
        plane_out[j] = jnp.concatenate(rows + [jnp.zeros((2, NK), F32)], axis=0)


def border(coef, edge, part, plane, lo, hi, faces, ghost_w, edge_w, face_w, flip_w):
    return pl.pallas_call(
        border_kernel,
        out_shape=[
            pltpu.VMEM((NJ, 32, NK), BF16),
            pltpu.VMEM((2, LN, NK), F32),
            pltpu.VMEM((NJ, 8, NK), F32),
        ],
        in_specs=[SM, SM] + [VM] * 9,
        out_specs=[VM] * 3,
        scratch_shapes=[pltpu.VMEM((NJ + 4, 8, NK), F32), pltpu.VMEM((2 * LN, NK), BF16)],
        compiler_params=params(4),
        name="border",
    )(coef, edge, part, plane, lo, hi, faces, ghost_w, edge_w, face_w, flip_w)


def finish_kernel(
    coef, part, plane, lo, hi, faces, ghost_w, face_w, flip_w, out, window, stack, held, sems
):
    fill_window(window, lo, hi, plane)

    def copies(step, slot):
        rows = pl.ds(step * BLOCK, BLOCK)
        return [
            pltpu.make_async_copy(held.at[slot, h], out.at[:, rows, lanes(h)], sems.at[slot, h])
            for h in range(2)
        ]

    def keep(slot, n, value):
        for h in range(2):
            half = held.at[slot, h].reshape(LN * BLOCK, HALF)
            half[pl.ds(n, LN, stride=BLOCK), :] = value[:, h * HALF : (h + 1) * HALF]

    for step in range(STEPS):
        slot = step % 2
        if step >= 2:
            for copy in copies(step - 2, slot):
                copy.wait()
        for n in range(BLOCK):
            j = step * BLOCK + n
            value = part[j] + mul(ghost_w[...], blend_ghosts(coef, window, j))
            if j == 0:
                value = value + turned_face(faces.at[1], stack, face_w, flip_w)
            if j == NJ - 1:
                value = value + turned_face(faces.at[0], stack, face_w, flip_w)
            keep(slot, n, value)
        for copy in copies(step, slot):
            copy.start()
    for step in range(STEPS - 2, STEPS):
        for copy in copies(step, step % 2):
            copy.wait()


def finish(coef, part, plane, lo, hi, faces, ghost_w, face_w, flip_w):
    return pl.pallas_call(
        finish_kernel,
        out_shape=jax.ShapeDtypeStruct((LN, NJ, NK), F32),
        in_specs=[SM] + [VM] * 8,
        out_specs=ANY,
        scratch_shapes=[
            pltpu.VMEM((NJ + 4, 8, NK), F32),
            pltpu.VMEM((2 * LN, NK), BF16),
            pltpu.VMEM((2, 2, LN, BLOCK, HALF), F32),
            pltpu.SemaphoreType.DMA((2, 2)),
        ],
        compiler_params=params(8),
        name="finish",
    )(coef, part, plane, lo, hi, faces, ghost_w, face_w, flip_w)


def exchange(faces, plane, bit, blocks):
    def across(step):
        return [
            (r * blocks + b, (1 - r) * blocks + (b + step) % blocks)
            for r in range(2)
            for b in range(blocks)
        ]

    axes = ("row", "blk")
    other = lax.ppermute(plane, "row", [(0, 1), (1, 0)])
    lo = lax.ppermute(plane[NJ - 2 :], axes, across(1))
    hi = lax.ppermute(plane[:2], axes, across(-1))
    got = [lax.ppermute(faces, "blk", [(b, b ^ (1 << k)) for b in range(blocks)]) for k in range(3)]
    received = jnp.where(bit == 0, got[0], jnp.where(bit == 1, got[1], got[2]))
    return other, lo, hi, received


def body(flow_state, forcing, stiffness, advection, line_inverse, margin_rows, margin_weights, partner_bit, turn_code):
    blocks = lax.axis_size("blk")
    row = lax.axis_index("row")
    bit = partner_bit[0, 0]
    state = in_hbm(flow_state.reshape(LN, NJ, NK))
    source = in_hbm(forcing.reshape(LN, NJ, NK))
    diagonal = in_hbm(stiffness.reshape(NI, NJ, NK))
    edge = jnp.where(row == 0, NI - 1, 0).reshape(1)
    comm = exchange(*begin(edge, state), bit, blocks)
    slots = margin_rows[0, 0] - jnp.arange(NJ, dtype=jnp.int32)[:, None]
    coef = jnp.sum(
        jnp.where(slots[..., None] == jnp.arange(5, dtype=jnp.int32), margin_weights[0, 0][..., None], 0.0), axis=1
    )
    flags = jnp.stack([row, turn_code[0, 0]])
    jac = jnp.pad(advection[0, 0], ((0, 2), (0, 2)))
    sweep_w, ghost_w, edge_w, face_w, flip_w = prepare(flags, line_inverse[0, 0], jac)
    sweep_w, coef = lax.optimization_barrier((sweep_w, coef))
    part = interior(state, source, diagonal, sweep_w)
    for sweep in range(SWEEPS - 1):
        ghosts, faces, plane = border(coef, edge, part, *comm, ghost_w, edge_w, face_w, flip_w)
        comm = exchange(faces, plane, bit, blocks)
        part = advance(part, ghosts, faces, source, diagonal, sweep_w, ghost_w)
    out = finish(coef, part, *comm, ghost_w, face_w, flip_w)
    return out.reshape(flow_state.shape)


def solution(mesh):
    return jax.shard_map(
        body,
        mesh=mesh,
        in_specs=(P("row", "blk"),) * 9,
        out_specs=P("row", "blk"),
        check_vma=False,
    )
```

```python
import functools

import jax
import jax.numpy as jnp
from jax import lax
from jax.experimental import pallas as pl
from jax.experimental.pallas import tpu as pltpu
from jax.sharding import PartitionSpec as P

SWEEPS = 3
NV, NI, NJ, NK = 6, 16, 64, 256
LN = NV * NI
F32, BF16 = jnp.float32, jnp.bfloat16
VM = pl.BlockSpec(memory_space=pltpu.VMEM)
SM = pl.BlockSpec(memory_space=pltpu.SMEM)
ANY = pl.BlockSpec(memory_space=pltpu.HBM)
HI = lax.Precision.HIGHEST
BLOCK = 8
REACH = 5
STEPS = NJ // BLOCK


def params(mib):
    return pltpu.CompilerParams(vmem_limit_bytes=mib << 20)


def in_hbm(x):
    return pltpu.with_memory_space_constraint(x, pltpu.HBM)


def iota(shape, dim):
    return lax.broadcasted_iota(jnp.int32, shape, dim)


def hot(mask):
    return jnp.where(mask, 1.0, 0.0).astype(F32)


def high_part(x):
    return x.astype(BF16).astype(F32)


def dot_exact(a, b):
    return jnp.dot(a, b, precision=HI, preferred_element_type=F32)


def mul(a, b):
    return jnp.dot(a, b, preferred_element_type=F32)


def prepare_kernel(
    flags, inverse, jacobian, slots, shares, sweep_w, ghost_w, edge_w, face_w, flip_w, coef
):
    rotor = flags[0] == 0
    code = flags[1]
    lines = inverse[...]
    r, c = iota((LN, LN), 0), iota((LN, LN), 1)
    rv, ri, cv, ci = r // NI, r % NI, c // NI, c % NI
    expand = hot(iota((LN, 8), 0) // NI == iota((LN, 8), 1))
    collect = hot(iota((8, LN), 1) // NI == iota((8, LN), 0))
    flux = dot_exact(dot_exact(expand, jacobian[...]), collect)
    last = NI - 1
    self_above = jnp.logical_and(ri == last, ci == last)
    self_below = jnp.logical_and(ri == 0, ci == 0)
    is_rotor = jnp.where(rotor, 1.0, 0.0)
    above = hot(ci == ri + 1) + hot(self_above) * (1.0 - is_rotor)
    below = hot(ri == ci + 1) + hot(self_below) * is_rotor
    along = hot(rv == cv) * (above + below) - 0.5 * flux * (above - below)
    both = dot_exact(lines, along)
    sign = jnp.where(rotor, 1.0, -1.0)
    edge = jnp.where(rotor, last, 0)
    g_row, g_col = iota((LN, 8), 0), iota((LN, 8), 1)
    spread = hot(g_row % NI == edge) * (
        hot(jnp.logical_and(g_row // NI == g_col, g_col < NV))
        - 0.5 * sign * dot_exact(expand, jacobian[...])
    )
    ghost = dot_exact(lines, spread)
    turned = dot_exact(lines, hot(jnp.logical_and(rv == cv, ri + ci == last)))
    face = jnp.where(code % 2 == 1, turned, lines)

    def place(rows, cols, starts):
        k, m = iota((rows, cols), 0), iota((rows, cols), 1)
        total = hot(m == k + starts[0])
        for start in starts[1:]:
            total = total + hot(m == k + start)
        return total.astype(BF16)

    def put(matrix, where):
        return mul(matrix.astype(BF16), where)

    def split(matrix):
        top = high_part(matrix)
        return top, high_part(matrix - top)

    l_hi, l_lo = split(lines)
    b_hi, b_lo = split(both)
    width = 4 * LN
    sweep_w[:LN] = (
        put(l_hi, place(LN, width, (0, LN))) + put(b_hi, place(LN, width, (2 * LN, 3 * LN)))
    ).astype(BF16)
    sweep_w[LN:] = (
        put(l_lo, place(LN, width, (0,))) + put(b_lo, place(LN, width, (2 * LN,)))
    ).astype(BF16)
    g_hi, g_lo = split(ghost)
    full = put(g_hi, place(8, 32, (0, 8))) + put(g_lo, place(8, 32, (16,)))
    ghost_w[...] = full.astype(BF16)
    at_edge = iota((16, LN), 1) == NI * iota((16, LN), 0) + edge
    pick = hot(jnp.logical_and(at_edge, iota((16, LN), 0) < NV)).astype(BF16)
    edge_w[...] = mul(pick, full.astype(BF16)).astype(BF16)
    f_hi, f_lo = split(face)
    face_w[:LN] = put(f_hi, place(LN, 2 * LN, (0, LN))).astype(BF16)
    face_w[LN:] = put(f_lo, place(LN, 2 * LN, (0,))).astype(BF16)
    ones = jnp.ones((NJ, NK), F32)
    diagonal = iota((NJ, NJ), 0) == iota((NJ, NJ), 1)
    for d in range(REACH):
        hits = slots[...] == iota(slots.shape, 1) + d
        line = jnp.sum(jnp.where(hits, shares[...], 0.0), axis=0, keepdims=True)
        coef[d] = dot_exact(jnp.where(diagonal, line, 0.0), ones)
    a, b = iota((NK, NK), 0), iota((NK, NK), 1)
    mirrored = hot(a + b == NK - 1)
    flip_w[...] = jnp.where(code // 2 == 1, mirrored, hot(a == b)).astype(BF16)


def prepare(flags, inverse, jacobian, slots, shares):
    return pl.pallas_call(
        prepare_kernel,
        out_shape=[
            pltpu.VMEM((2 * LN, 4 * LN), BF16),
            pltpu.VMEM((LN, 32), BF16),
            pltpu.VMEM((16, 32), BF16),
            pltpu.VMEM((2 * LN, 2 * LN), BF16),
            pltpu.VMEM((NK, NK), BF16),
            pltpu.VMEM((REACH, NJ, NK), F32),
        ],
        in_specs=[SM, VM, VM, VM, VM],
        out_specs=[VM] * 6,
        compiler_params=params(6),
        name="prepare",
    )(flags, inverse, jacobian, slots, shares)


HALF = NK // 2


def lanes(h):
    return pl.ds(h * HALF, HALF)


def begin_kernel(edge, state, face_out, plane_out, ends, cut, sems):
    at = edge[0]
    copies = []
    for h in range(2):
        copies.append(pltpu.make_async_copy(state.at[:, 0:8, lanes(h)], ends.at[0, h], sems.at[0, h]))
        copies.append(pltpu.make_async_copy(state.at[:, NJ - 8 : NJ, lanes(h)], ends.at[1, h], sems.at[1, h]))
        for v in range(NV):
            copies.append(pltpu.make_async_copy(state.at[v * NI + at, :, lanes(h)], cut.at[h, v], sems.at[2 + v, h]))
    for copy in copies:
        copy.start()
    for copy in copies:
        copy.wait()
    pad = jnp.zeros((2, HALF), F32)
    for h in range(2):
        for side in range(2):
            rows = ends.at[side, h].reshape(LN * 8, HALF)
            face_out[side, :, lanes(h)] = rows[pl.ds(7 * side, LN, stride=8), :]
        planes = cut.at[h].reshape(NV * NJ, HALF)
        for j in range(NJ):
            plane_out[j, :, lanes(h)] = jnp.concatenate([planes[pl.ds(j, NV, stride=NJ), :], pad], axis=0)


def begin(edge, state):
    return pl.pallas_call(
        begin_kernel,
        out_shape=[pltpu.VMEM((2, LN, NK), F32), pltpu.VMEM((NJ, 8, NK), F32)],
        in_specs=[SM, ANY],
        out_specs=[VM] * 2,
        scratch_shapes=[
            pltpu.VMEM((2, 2, LN, 8, HALF), F32),
            pltpu.VMEM((2, NV, NJ, HALF), F32),
            pltpu.SemaphoreType.DMA((2 + NV, 2)),
        ],
        compiler_params=params(4),
        name="begin",
    )(edge, state)


def halves(x):
    top = x.astype(BF16)
    return top, (x - top.astype(F32)).astype(BF16)


def shifted(a, b):
    lane = iota(a.shape, 1)
    first, end = lane == 0, lane == HALF - 1
    ra, rb = pltpu.roll(a, 1, 1), pltpu.roll(b, 1, 1)
    la, lb = pltpu.roll(a, HALF - 1, 1), pltpu.roll(b, HALF - 1, 1)
    zero = jnp.zeros_like(a)
    left = jnp.where(first, zero, ra) + jnp.where(end, lb, la)
    right = jnp.where(first, ra, rb) + jnp.where(end, zero, lb)
    return left, right


def fetches(pairs, sems):
    def copies(step, slot):
        rows = pl.ds(step * BLOCK, BLOCK)
        return [
            pltpu.make_async_copy(array.at[:, rows, lanes(h)], place(step, slot, h), sems.at[n, h, slot])
            for n, (array, place) in enumerate(pairs)
            for h in range(2)
        ]

    def start(step, slot):
        for copy in copies(step, slot):
            copy.start()

    def wait(step, slot):
        for copy in copies(step, slot):
            copy.wait()

    return start, wait


def spaced(ref, h, n, v):
    half = ref.at[h].reshape(ref.shape[1] * BLOCK, HALF)
    return half[pl.ds(n + v * NI * BLOCK, NI, stride=BLOCK), :]


def relax(row, s_buf, d_buf, weights, out, stack):
    def gather(step, slot):
        for n in range(BLOCK):
            d = [spaced(d_buf.at[slot], h, n, 0) for h in range(2)]
            for v in range(NV):
                pair = [row(step, n, v, h) for h in range(2)]
                along = shifted(*pair)
                for h in range(2):
                    s = pair[h]
                    if n == 0:
                        below = row(jnp.maximum(step - 1, 0), BLOCK - 1, v, h)
                        below = below * jnp.where(step == 0, 0.0, 1.0)
                    else:
                        below = row(step, n - 1, v, h)
                    if n == BLOCK - 1:
                        above = row(jnp.minimum(step + 1, STEPS - 1), 0, v, h)
                        above = above * jnp.where(step == STEPS - 1, 0.0, 1.0)
                    else:
                        above = row(step, n + 1, v, h)
                    e = spaced(s_buf.at[slot], h, n, v) - d[h] * s + (below + above) + along[h]
                    for k, value in enumerate(halves(e) + halves(s)):
                        stack[slot, n, k * LN + v * NI : k * LN + (v + 1) * NI, lanes(h)] = value

    def solve(step, slot):
        for n in range(BLOCK):
            both = mul(weights[...], stack[slot, n])
            for v in range(NV):
                at = v * NI
                change = both[at : at + NI] + both[LN + at : LN + at + NI]
                for h in range(2):
                    piece = change[:, h * HALF : (h + 1) * HALF]
                    out[step * BLOCK + n, h, at : at + NI] = row(step, n, v, h) + piece

    return gather, solve


def blend_ghosts(coef, window, j):
    total = coef[0, pl.ds(j, 1), :] * window[j]
    for d in range(1, REACH):
        total = total + coef[d, pl.ds(j, 1), :] * window[j + d]
    g_hi = high_part(total)
    g_lo = high_part(total - g_hi)
    return jnp.concatenate([g_hi, g_lo, g_hi, jnp.zeros_like(g_hi)], axis=0).astype(BF16)


def fill_window(window, lo, hi, plane):
    window[0:2] = lo[...]
    window[2 : NJ + 2] = plane[...]
    window[NJ + 2 :] = hi[...]


def turned_face(face, stack, face_w, flip_w):
    f_hi, f_lo = halves(face[...])
    stack[:LN] = f_hi
    stack[LN:] = f_lo
    both = mul(face_w[...], mul(stack[...], flip_w[...]).astype(BF16))
    return both[:LN] + both[LN:]


PART = (NJ, 2, LN, HALF)


def interior_kernel(state, source, diagonal, weights, out, stack, s_buf, d_buf, sems, held, more):
    start, wait = fetches(
        [
            (source, lambda step, slot, h: s_buf.at[slot, h]),
            (diagonal, lambda step, slot, h: d_buf.at[slot, h]),
        ],
        sems,
    )

    def load(step):
        rows = pl.ds(step * BLOCK, BLOCK)
        return [
            pltpu.make_async_copy(state.at[:, rows, lanes(h)], held.at[step, h], more.at[h, step])
            for h in range(2)
        ]

    def arrived(step):
        for copy in load(step):
            copy.wait()

    def row(step, n, v, h):
        return spaced(held.at[step], h, n, v)

    gather, solve = relax(row, s_buf, d_buf, weights, out, stack)
    for step in range(STEPS):
        for copy in load(step):
            copy.start()
        if step < 2:
            start(step, step)
    arrived(0)
    arrived(1)
    wait(0, 0)
    gather(0, 0)
    wait(1, 1)

    def pair(step, carry):
        first = 2 * step

        @pl.when(first + 2 < STEPS)
        def _():
            start(first + 2, 0)
            arrived(first + 2)

        gather(first + 1, 1)
        solve(first, 0)

        @pl.when(first + 2 < STEPS)
        def _():
            start(first + 3, 1)
            arrived(first + 3)
            wait(first + 2, 0)

        gather(jnp.minimum(first + 2, STEPS - 1), 0)
        solve(first + 1, 1)

        @pl.when(first + 2 < STEPS)
        def _():
            wait(first + 3, 1)

        return carry

    lax.fori_loop(0, STEPS // 2, pair, 0)


RELAX_SCRATCH = [
    pltpu.VMEM((2, BLOCK, 4 * LN, NK), BF16),
    pltpu.VMEM((2, 2, LN, BLOCK, HALF), F32),
    pltpu.VMEM((2, 2, NI, BLOCK, HALF), F32),
    pltpu.SemaphoreType.DMA((2, 2, 2)),
]
RELAX_COST = pl.CostEstimate(flops=4_800_000_000, bytes_accessed=14_000_000, transcendentals=0)


def interior(state, source, diagonal, weights):
    return pl.pallas_call(
        interior_kernel,
        out_shape=pltpu.VMEM(PART, F32),
        in_specs=[ANY, ANY, ANY, VM],
        out_specs=VM,
        scratch_shapes=RELAX_SCRATCH
        + [pltpu.VMEM((STEPS, 2, LN, BLOCK, HALF), F32), pltpu.SemaphoreType.DMA((2, STEPS))],
        compiler_params=params(16),
        cost_estimate=RELAX_COST,
        name="interior",
    )(state, source, diagonal, weights)


def advance_kernel(part, ghosts, faces, source, diagonal, weights, ghost_w, out, stack, s_buf, d_buf, sems, fresh):
    start, wait = fetches(
        [
            (source, lambda step, slot, h: s_buf.at[slot, h]),
            (diagonal, lambda step, slot, h: d_buf.at[slot, h]),
        ],
        sems,
    )

    def fix(step):
        for n in range(BLOCK):
            j = step * BLOCK + n
            change = mul(ghost_w[...], ghosts[j])
            for h in range(2):
                value = part[j, h] + change[:, h * HALF : (h + 1) * HALF]
                if n == BLOCK - 1:
                    value = jnp.where(j == NJ - 1, faces[1, :, lanes(h)], value)
                fresh[j, h] = value

    def row(step, n, v, h):
        return fresh[step * BLOCK + n, h, v * NI : (v + 1) * NI]

    gather, solve = relax(row, s_buf, d_buf, weights, out, stack)
    start(0, 0)
    start(1, 1)

    def early(step, carry):
        fix(step)
        return carry

    lax.fori_loop(0, 3, early, 0)
    for h in range(2):
        fresh[0, h] = faces[0, :, lanes(h)]
    wait(0, 0)
    gather(0, 0)
    wait(1, 1)

    def pair(step, carry):
        first = 2 * step

        @pl.when(first + 2 < STEPS)
        def _():
            start(first + 2, 0)

        fix(jnp.minimum(first + 3, STEPS - 1))
        gather(first + 1, 1)
        solve(first, 0)

        @pl.when(first + 2 < STEPS)
        def _():
            start(first + 3, 1)
            wait(first + 2, 0)

        fix(jnp.minimum(first + 4, STEPS - 1))
        gather(jnp.minimum(first + 2, STEPS - 1), 0)
        solve(first + 1, 1)

        @pl.when(first + 2 < STEPS)
        def _():
            wait(first + 3, 1)

        return carry

    lax.fori_loop(0, STEPS // 2, pair, 0)


def advance(part, ghosts, faces, source, diagonal, weights, ghost_w):
    return pl.pallas_call(
        advance_kernel,
        out_shape=pltpu.VMEM(PART, F32),
        in_specs=[VM, VM, VM, ANY, ANY, VM, VM],
        out_specs=VM,
        scratch_shapes=RELAX_SCRATCH + [pltpu.VMEM(PART, F32)],
        compiler_params=params(16),
        cost_estimate=RELAX_COST,
        name="advance",
    )(part, ghosts, faces, source, diagonal, weights, ghost_w)


def border_kernel(
    coef, edge, part, plane, lo, hi, faces, ghost_w, edge_w, face_w, flip_w,
    ghosts, face_out, plane_out, window, stack, kept,
):
    fill_window(window, lo, hi, plane)
    at = edge[0]

    pad = jnp.zeros((2, HALF), F32)

    def block(step, carry):
        for n in range(2 * BLOCK):
            j = step * 2 * BLOCK + n
            g = blend_ghosts(coef, window, j)
            ghosts[j] = g
            change = mul(edge_w[...], g)
            for h in range(2):
                old = jnp.concatenate([part[j, h, pl.ds(at, NV, stride=NI), :], pad], axis=0)
                plane_out[j, :, lanes(h)] = old + change[:8, h * HALF : (h + 1) * HALF]
        return carry

    lax.fori_loop(0, STEPS // 2, block, 0)
    for side, j in ((0, 0), (1, NJ - 1)):
        change = turned_face(faces.at[1 - side], stack, face_w, flip_w) + mul(ghost_w[...], ghosts[j])
        for h in range(2):
            kept[h] = part[j, h] + change[:, h * HALF : (h + 1) * HALF]
            face_out[side, :, lanes(h)] = kept[h]
            rows = jnp.concatenate([kept[h, pl.ds(at, NV, stride=NI), :], pad], axis=0)
            plane_out[j, :, lanes(h)] = rows


def border(coef, edge, part, plane, lo, hi, faces, ghost_w, edge_w, face_w, flip_w):
    return pl.pallas_call(
        border_kernel,
        out_shape=[
            pltpu.VMEM((NJ, 32, NK), BF16),
            pltpu.VMEM((2, LN, NK), F32),
            pltpu.VMEM((NJ, 8, NK), F32),
        ],
        in_specs=[VM, SM] + [VM] * 9,
        out_specs=[VM] * 3,
        scratch_shapes=[
            pltpu.VMEM((NJ + 4, 8, NK), F32),
            pltpu.VMEM((2 * LN, NK), BF16),
            pltpu.VMEM((2, LN, HALF), F32),
        ],
        compiler_params=params(4),
        name="border",
    )(coef, edge, part, plane, lo, hi, faces, ghost_w, edge_w, face_w, flip_w)


def finish_kernel(
    coef, part, plane, lo, hi, faces, ghost_w, face_w, flip_w, out, window, stack, held, sems
):
    fill_window(window, lo, hi, plane)

    def copies(step, slot):
        rows = pl.ds(step * BLOCK, BLOCK)
        return [
            pltpu.make_async_copy(held.at[slot, h], out.at[:, rows, lanes(h)], sems.at[slot, h])
            for h in range(2)
        ]

    def keep(slot, n, j, change):
        for h in range(2):
            half = held.at[slot, h].reshape(LN * BLOCK, HALF)
            half[pl.ds(n, LN, stride=BLOCK), :] = part[j, h] + change[:, h * HALF : (h + 1) * HALF]

    first = turned_face(faces.at[1], stack, face_w, flip_w)
    last = turned_face(faces.at[0], stack, face_w, flip_w)

    def pair(step, carry):
        for slot in range(2):
            at = 2 * step + slot

            @pl.when(step > 0)
            def _():
                for copy in copies(at - 2, slot):
                    copy.wait()

            for n in range(BLOCK):
                j = at * BLOCK + n
                change = mul(ghost_w[...], blend_ghosts(coef, window, j))
                if n == 0 and slot == 0:
                    change = change + first * jnp.where(step == 0, 1.0, 0.0)
                if n == BLOCK - 1 and slot == 1:
                    change = change + last * jnp.where(step == STEPS // 2 - 1, 1.0, 0.0)
                keep(slot, n, j, change)
            for copy in copies(at, slot):
                copy.start()
        return carry

    lax.fori_loop(0, STEPS // 2, pair, 0)
    for step in range(STEPS - 2, STEPS):
        for copy in copies(step, step % 2):
            copy.wait()


def finish(coef, part, plane, lo, hi, faces, ghost_w, face_w, flip_w):
    return pl.pallas_call(
        finish_kernel,
        out_shape=jax.ShapeDtypeStruct((LN, NJ, NK), F32),
        in_specs=[VM] * 9,
        out_specs=ANY,
        scratch_shapes=[
            pltpu.VMEM((NJ + 4, 8, NK), F32),
            pltpu.VMEM((2 * LN, NK), BF16),
            pltpu.VMEM((2, 2, LN, BLOCK, HALF), F32),
            pltpu.SemaphoreType.DMA((2, 2)),
        ],
        compiler_params=params(8),
        name="finish",
    )(coef, part, plane, lo, hi, faces, ghost_w, face_w, flip_w)


def exchange(plane, blocks):
    def across(step):
        return [
            (r * blocks + b, (1 - r) * blocks + (b + step) % blocks)
            for r in range(2)
            for b in range(blocks)
        ]

    axes = ("row", "blk")
    other = lax.ppermute(plane, "row", [(0, 1), (1, 0)])
    lo = lax.ppermute(plane[NJ - 2 :], axes, across(1))
    hi = lax.ppermute(plane[:2], axes, across(-1))
    return other, lo, hi


def beside(faces, bit, blocks, work, *operands):
    def branch(k):
        def run(faces, *operands):
            received = lax.ppermute(faces, "blk", [(b, b ^ (1 << k)) for b in range(blocks)])
            return received, work(*operands)

        return run

    return lax.switch(bit, [branch(k) for k in range(3)], faces, *operands)


def body(flow_state, forcing, stiffness, advection, line_inverse, margin_rows, margin_weights, partner_bit, turn_code):
    blocks = lax.axis_size("blk")
    row = lax.axis_index("row")
    bit = partner_bit[0, 0]
    state = in_hbm(flow_state.reshape(LN, NJ, NK))
    source = in_hbm(forcing.reshape(LN, NJ, NK))
    diagonal = in_hbm(stiffness.reshape(NI, NJ, NK))
    edge = jnp.where(row == 0, NI - 1, 0).reshape(1)
    faces, plane = begin(edge, state)
    comm = exchange(plane, blocks)
    flags = jnp.stack([row, turn_code[0, 0]])
    jac = jnp.pad(advection[0, 0], ((0, 2), (0, 2)))
    sweep_w, ghost_w, edge_w, face_w, flip_w, coef = prepare(
        flags, line_inverse[0, 0], jac, margin_rows[0, 0].T, margin_weights[0, 0].T
    )
    received, part = beside(faces, bit, blocks, interior, state, source, diagonal, sweep_w)
    for sweep in range(SWEEPS - 1):
        ghosts, faces, plane = border(
            coef, edge, part, *comm, received, ghost_w, edge_w, face_w, flip_w
        )
        comm = exchange(plane, blocks)
        received, part = beside(
            faces, bit, blocks, advance, part, ghosts, faces, source, diagonal, sweep_w, ghost_w
        )
    out = finish(coef, part, *comm, received, ghost_w, face_w, flip_w)
    return out.reshape(flow_state.shape)


def solution(mesh):
    return jax.shard_map(
        body,
        mesh=mesh,
        in_specs=(P("row", "blk"),) * 9,
        out_specs=P("row", "blk"),
        check_vma=False,
    )
```

```python
import functools

import jax
import jax.numpy as jnp
from jax import lax
from jax.experimental import pallas as pl
from jax.experimental.pallas import tpu as pltpu
from jax.sharding import PartitionSpec as P

SWEEPS = 3
NV, NI, NJ, NK = 6, 16, 64, 256
LN = NV * NI
F32, BF16 = jnp.float32, jnp.bfloat16
VM = pl.BlockSpec(memory_space=pltpu.VMEM)
SM = pl.BlockSpec(memory_space=pltpu.SMEM)
ANY = pl.BlockSpec(memory_space=pltpu.HBM)
HI = lax.Precision.HIGHEST
BLOCK = 8
REACH = 5
STEPS = NJ // BLOCK


def params(mib):
    return pltpu.CompilerParams(vmem_limit_bytes=mib << 20)


def in_hbm(x):
    return pltpu.with_memory_space_constraint(x, pltpu.HBM)


def iota(shape, dim):
    return lax.broadcasted_iota(jnp.int32, shape, dim)


def hot(mask):
    return jnp.where(mask, 1.0, 0.0).astype(F32)


def high_part(x):
    return x.astype(BF16).astype(F32)


def dot_exact(a, b):
    return jnp.dot(a, b, precision=HI, preferred_element_type=F32)


def mul(a, b):
    return jnp.dot(a, b, preferred_element_type=F32)


def prepare_kernel(
    flags, inverse, jacobian, slots, shares, sweep_w, ghost_w, edge_w, face_w, flip_w, coef
):
    rotor = flags[0] == 0
    code = flags[1]
    lines = inverse[...]
    r, c = iota((LN, LN), 0), iota((LN, LN), 1)
    rv, ri, cv, ci = r // NI, r % NI, c // NI, c % NI
    expand = hot(iota((LN, 8), 0) // NI == iota((LN, 8), 1))
    collect = hot(iota((8, LN), 1) // NI == iota((8, LN), 0))
    flux = dot_exact(dot_exact(expand, jacobian[...]), collect)
    last = NI - 1
    self_above = jnp.logical_and(ri == last, ci == last)
    self_below = jnp.logical_and(ri == 0, ci == 0)
    is_rotor = jnp.where(rotor, 1.0, 0.0)
    above = hot(ci == ri + 1) + hot(self_above) * (1.0 - is_rotor)
    below = hot(ri == ci + 1) + hot(self_below) * is_rotor
    along = hot(rv == cv) * (above + below) - 0.5 * flux * (above - below)
    both = dot_exact(lines, along)
    sign = jnp.where(rotor, 1.0, -1.0)
    edge = jnp.where(rotor, last, 0)
    g_row, g_col = iota((LN, 8), 0), iota((LN, 8), 1)
    spread = hot(g_row % NI == edge) * (
        hot(jnp.logical_and(g_row // NI == g_col, g_col < NV))
        - 0.5 * sign * dot_exact(expand, jacobian[...])
    )
    ghost = dot_exact(lines, spread)
    turned = dot_exact(lines, hot(jnp.logical_and(rv == cv, ri + ci == last)))
    face = jnp.where(code % 2 == 1, turned, lines)

    def place(rows, cols, starts):
        k, m = iota((rows, cols), 0), iota((rows, cols), 1)
        total = hot(m == k + starts[0])
        for start in starts[1:]:
            total = total + hot(m == k + start)
        return total.astype(BF16)

    def put(matrix, where):
        return mul(matrix.astype(BF16), where)

    def split(matrix):
        top = high_part(matrix)
        return top, high_part(matrix - top)

    l_hi, l_lo = split(lines)
    b_hi, b_lo = split(both)
    width = 4 * LN
    sweep_w[:LN] = (
        put(l_hi, place(LN, width, (0, LN))) + put(b_hi, place(LN, width, (2 * LN, 3 * LN)))
    ).astype(BF16)
    sweep_w[LN:] = (
        put(l_lo, place(LN, width, (0,))) + put(b_lo, place(LN, width, (2 * LN,)))
    ).astype(BF16)
    g_hi, g_lo = split(ghost)
    full = put(g_hi, place(8, 32, (0, 8))) + put(g_lo, place(8, 32, (16,)))
    ghost_w[...] = full.astype(BF16)
    at_edge = iota((16, LN), 1) == NI * iota((16, LN), 0) + edge
    pick = hot(jnp.logical_and(at_edge, iota((16, LN), 0) < NV)).astype(BF16)
    edge_w[...] = mul(pick, full.astype(BF16)).astype(BF16)
    f_hi, f_lo = split(face)
    face_w[:LN] = put(f_hi, place(LN, 2 * LN, (0, LN))).astype(BF16)
    face_w[LN:] = put(f_lo, place(LN, 2 * LN, (0,))).astype(BF16)
    ones = jnp.ones((NJ, NK), F32)
    diagonal = iota((NJ, NJ), 0) == iota((NJ, NJ), 1)
    for d in range(REACH):
        hits = slots[...] == iota(slots.shape, 1) + d
        line = jnp.sum(jnp.where(hits, shares[...], 0.0), axis=0, keepdims=True)
        coef[d] = dot_exact(jnp.where(diagonal, line, 0.0), ones)
    a, b = iota((NK, NK), 0), iota((NK, NK), 1)
    mirrored = hot(a + b == NK - 1)
    flip_w[...] = jnp.where(code // 2 == 1, mirrored, hot(a == b)).astype(BF16)


def prepare(flags, inverse, jacobian, slots, shares):
    return pl.pallas_call(
        prepare_kernel,
        out_shape=[
            pltpu.VMEM((2 * LN, 4 * LN), BF16),
            pltpu.VMEM((LN, 32), BF16),
            pltpu.VMEM((16, 32), BF16),
            pltpu.VMEM((2 * LN, 2 * LN), BF16),
            pltpu.VMEM((NK, NK), BF16),
            pltpu.VMEM((REACH, NJ, NK), F32),
        ],
        in_specs=[SM, VM, VM, VM, VM],
        out_specs=[VM] * 6,
        compiler_params=params(6),
        name="prepare",
    )(flags, inverse, jacobian, slots, shares)


HALF = NK // 2


def lanes(h):
    return pl.ds(h * HALF, HALF)


def begin_kernel(edge, state, face_out, plane_out, ends, cut, sems):
    at = edge[0]
    copies = []
    for h in range(2):
        copies.append(pltpu.make_async_copy(state.at[:, 0:8, lanes(h)], ends.at[0, h], sems.at[0, h]))
        copies.append(pltpu.make_async_copy(state.at[:, NJ - 8 : NJ, lanes(h)], ends.at[1, h], sems.at[1, h]))
        for v in range(NV):
            copies.append(pltpu.make_async_copy(state.at[v * NI + at, :, lanes(h)], cut.at[h, v], sems.at[2 + v, h]))
    for copy in copies:
        copy.start()
    for copy in copies:
        copy.wait()
    pad = jnp.zeros((2, HALF), F32)
    for h in range(2):
        for side in range(2):
            rows = ends.at[side, h].reshape(LN * 8, HALF)
            face_out[side, :, lanes(h)] = rows[pl.ds(7 * side, LN, stride=8), :]
        planes = cut.at[h].reshape(NV * NJ, HALF)
        for j in range(NJ):
            plane_out[j, :, lanes(h)] = jnp.concatenate([planes[pl.ds(j, NV, stride=NJ), :], pad], axis=0)


def begin(edge, state):
    return pl.pallas_call(
        begin_kernel,
        out_shape=[pltpu.VMEM((2, LN, NK), F32), pltpu.VMEM((NJ, 8, NK), F32)],
        in_specs=[SM, ANY],
        out_specs=[VM] * 2,
        scratch_shapes=[
            pltpu.VMEM((2, 2, LN, 8, HALF), F32),
            pltpu.VMEM((2, NV, NJ, HALF), F32),
            pltpu.SemaphoreType.DMA((2 + NV, 2)),
        ],
        compiler_params=params(4),
        name="begin",
    )(edge, state)


def halves(x):
    top = x.astype(BF16)
    return top, (x - top.astype(F32)).astype(BF16)


def shifted(a, b):
    lane = iota(a.shape, 1)
    first, end = lane == 0, lane == HALF - 1
    ra, rb = pltpu.roll(a, 1, 1), pltpu.roll(b, 1, 1)
    la, lb = pltpu.roll(a, HALF - 1, 1), pltpu.roll(b, HALF - 1, 1)
    zero = jnp.zeros_like(a)
    left = jnp.where(first, zero, ra) + jnp.where(end, lb, la)
    right = jnp.where(first, ra, rb) + jnp.where(end, zero, lb)
    return left, right


def fetches(pairs, sems):
    def copies(step, slot):
        rows = pl.ds(step * BLOCK, BLOCK)
        return [
            pltpu.make_async_copy(array.at[:, rows, lanes(h)], place(step, slot, h), sems.at[n, h, slot])
            for n, (array, place) in enumerate(pairs)
            for h in range(2)
        ]

    def start(step, slot):
        for copy in copies(step, slot):
            copy.start()

    def wait(step, slot):
        for copy in copies(step, slot):
            copy.wait()

    return start, wait


def spaced(ref, h, n, v):
    half = ref.at[h].reshape(ref.shape[1] * BLOCK, HALF)
    return half[pl.ds(n + v * NI * BLOCK, NI, stride=BLOCK), :]


def relax(row, s_buf, d_buf, weights, out, stack):
    def gather(step, slot):
        for n in range(BLOCK):
            d = [spaced(d_buf.at[slot], h, n, 0) for h in range(2)]
            for v in range(NV):
                pair = [row(step, n, v, h) for h in range(2)]
                along = shifted(*pair)
                for h in range(2):
                    s = pair[h]
                    if n == 0:
                        below = row(jnp.maximum(step - 1, 0), BLOCK - 1, v, h)
                        below = below * jnp.where(step == 0, 0.0, 1.0)
                    else:
                        below = row(step, n - 1, v, h)
                    if n == BLOCK - 1:
                        above = row(jnp.minimum(step + 1, STEPS - 1), 0, v, h)
                        above = above * jnp.where(step == STEPS - 1, 0.0, 1.0)
                    else:
                        above = row(step, n + 1, v, h)
                    e = spaced(s_buf.at[slot], h, n, v) - d[h] * s + (below + above) + along[h]
                    for k, value in enumerate(halves(e) + halves(s)):
                        stack[slot, n, k * LN + v * NI : k * LN + (v + 1) * NI, lanes(h)] = value

    def solve(step, slot):
        for n in range(BLOCK):
            both = mul(weights[...], stack[slot, n])
            for v in range(NV):
                at = v * NI
                change = both[at : at + NI] + both[LN + at : LN + at + NI]
                for h in range(2):
                    piece = change[:, h * HALF : (h + 1) * HALF]
                    out[step * BLOCK + n, h, at : at + NI] = row(step, n, v, h) + piece

    return gather, solve


def blend_ghosts(coef, window, j):
    total = coef[0, pl.ds(j, 1), :] * window[j]
    for d in range(1, REACH):
        total = total + coef[d, pl.ds(j, 1), :] * window[j + d]
    g_hi = high_part(total)
    g_lo = high_part(total - g_hi)
    return jnp.concatenate([g_hi, g_lo, g_hi, jnp.zeros_like(g_hi)], axis=0).astype(BF16)


def fill_window(window, lo, hi, plane):
    window[0:2] = lo[...]
    window[2 : NJ + 2] = plane[...]
    window[NJ + 2 :] = hi[...]


def turned_face(face, stack, face_w, flip_w):
    f_hi, f_lo = halves(face[...])
    stack[:LN] = f_hi
    stack[LN:] = f_lo
    both = mul(face_w[...], mul(stack[...], flip_w[...]).astype(BF16))
    return both[:LN] + both[LN:]


PART = (NJ, 2, LN, HALF)


def interior_kernel(state, source, diagonal, weights, out, stack, s_buf, d_buf, sems, held, more):
    start, wait = fetches(
        [
            (source, lambda step, slot, h: s_buf.at[slot, h]),
            (diagonal, lambda step, slot, h: d_buf.at[slot, h]),
        ],
        sems,
    )

    def load(step):
        rows = pl.ds(step * BLOCK, BLOCK)
        return [
            pltpu.make_async_copy(state.at[:, rows, lanes(h)], held.at[step, h], more.at[h, step])
            for h in range(2)
        ]

    def arrived(step):
        for copy in load(step):
            copy.wait()

    def row(step, n, v, h):
        return spaced(held.at[step], h, n, v)

    gather, solve = relax(row, s_buf, d_buf, weights, out, stack)
    for step in range(STEPS):
        for copy in load(step):
            copy.start()
        if step < 2:
            start(step, step)
    arrived(0)
    arrived(1)
    wait(0, 0)
    gather(0, 0)
    wait(1, 1)

    def pair(step, carry):
        first = 2 * step

        @pl.when(first + 2 < STEPS)
        def _():
            start(first + 2, 0)
            arrived(first + 2)

        gather(first + 1, 1)
        solve(first, 0)

        @pl.when(first + 2 < STEPS)
        def _():
            start(first + 3, 1)
            arrived(first + 3)
            wait(first + 2, 0)

        gather(jnp.minimum(first + 2, STEPS - 1), 0)
        solve(first + 1, 1)

        @pl.when(first + 2 < STEPS)
        def _():
            wait(first + 3, 1)

        return carry

    lax.fori_loop(0, STEPS // 2, pair, 0)


RELAX_SCRATCH = [
    pltpu.VMEM((2, BLOCK, 4 * LN, NK), BF16),
    pltpu.VMEM((2, 2, LN, BLOCK, HALF), F32),
    pltpu.VMEM((2, 2, NI, BLOCK, HALF), F32),
    pltpu.SemaphoreType.DMA((2, 2, 2)),
]
RELAX_COST = pl.CostEstimate(flops=4_800_000_000, bytes_accessed=14_000_000, transcendentals=0)


def interior(state, source, diagonal, weights):
    return pl.pallas_call(
        interior_kernel,
        out_shape=pltpu.VMEM(PART, F32),
        in_specs=[ANY, ANY, ANY, VM],
        out_specs=VM,
        scratch_shapes=RELAX_SCRATCH
        + [pltpu.VMEM((STEPS, 2, LN, BLOCK, HALF), F32), pltpu.SemaphoreType.DMA((2, STEPS))],
        compiler_params=params(16),
        cost_estimate=RELAX_COST,
        name="interior",
    )(state, source, diagonal, weights)


def advance_kernel(part, ghosts, faces, source, diagonal, weights, ghost_w, out, stack, s_buf, d_buf, sems, fresh):
    start, wait = fetches(
        [
            (source, lambda step, slot, h: s_buf.at[slot, h]),
            (diagonal, lambda step, slot, h: d_buf.at[slot, h]),
        ],
        sems,
    )

    def fix(step):
        for n in range(BLOCK):
            j = step * BLOCK + n
            change = mul(ghost_w[...], ghosts[j])
            for h in range(2):
                value = part[j, h] + change[:, h * HALF : (h + 1) * HALF]
                if n == BLOCK - 1:
                    value = jnp.where(j == NJ - 1, faces[1, :, lanes(h)], value)
                fresh[j, h] = value

    def row(step, n, v, h):
        return fresh[step * BLOCK + n, h, v * NI : (v + 1) * NI]

    gather, solve = relax(row, s_buf, d_buf, weights, out, stack)
    start(0, 0)
    start(1, 1)

    def early(step, carry):
        fix(step)
        return carry

    lax.fori_loop(0, 3, early, 0)
    for h in range(2):
        fresh[0, h] = faces[0, :, lanes(h)]
    wait(0, 0)
    gather(0, 0)
    wait(1, 1)

    def pair(step, carry):
        first = 2 * step

        @pl.when(first + 2 < STEPS)
        def _():
            start(first + 2, 0)

        fix(jnp.minimum(first + 3, STEPS - 1))
        gather(first + 1, 1)
        solve(first, 0)

        @pl.when(first + 2 < STEPS)
        def _():
            start(first + 3, 1)
            wait(first + 2, 0)

        fix(jnp.minimum(first + 4, STEPS - 1))
        gather(jnp.minimum(first + 2, STEPS - 1), 0)
        solve(first + 1, 1)

        @pl.when(first + 2 < STEPS)
        def _():
            wait(first + 3, 1)

        return carry

    lax.fori_loop(0, STEPS // 2, pair, 0)


def advance(part, ghosts, faces, source, diagonal, weights, ghost_w):
    return pl.pallas_call(
        advance_kernel,
        out_shape=pltpu.VMEM(PART, F32),
        in_specs=[VM, VM, VM, ANY, ANY, VM, VM],
        out_specs=VM,
        scratch_shapes=RELAX_SCRATCH + [pltpu.VMEM(PART, F32)],
        compiler_params=params(16),
        cost_estimate=RELAX_COST,
        name="advance",
    )(part, ghosts, faces, source, diagonal, weights, ghost_w)


def border_kernel(
    coef, edge, part, plane, lo, hi, faces, ghost_w, edge_w, face_w, flip_w,
    ghosts, face_out, plane_out, window, stack, kept, near, sem,
):
    brought = pltpu.make_async_copy(faces, near, sem)
    brought.start()
    fill_window(window, lo, hi, plane)
    at = edge[0]

    pad = jnp.zeros((2, HALF), F32)

    def block(step, carry):
        for n in range(2 * BLOCK):
            j = step * 2 * BLOCK + n
            g = blend_ghosts(coef, window, j)
            ghosts[j] = g
            change = mul(edge_w[...], g)
            for h in range(2):
                old = jnp.concatenate([part[j, h, pl.ds(at, NV, stride=NI), :], pad], axis=0)
                plane_out[j, :, lanes(h)] = old + change[:8, h * HALF : (h + 1) * HALF]
        return carry

    lax.fori_loop(0, STEPS // 2, block, 0)
    brought.wait()
    for side, j in ((0, 0), (1, NJ - 1)):
        change = turned_face(near.at[1 - side], stack, face_w, flip_w) + mul(ghost_w[...], ghosts[j])
        for h in range(2):
            kept[h] = part[j, h] + change[:, h * HALF : (h + 1) * HALF]
            face_out[side, :, lanes(h)] = kept[h]
            rows = jnp.concatenate([kept[h, pl.ds(at, NV, stride=NI), :], pad], axis=0)
            plane_out[j, :, lanes(h)] = rows


def border(coef, edge, part, plane, lo, hi, faces, ghost_w, edge_w, face_w, flip_w):
    return pl.pallas_call(
        border_kernel,
        out_shape=[
            pltpu.VMEM((NJ, 32, NK), BF16),
            pltpu.VMEM((2, LN, NK), F32),
            pltpu.VMEM((NJ, 8, NK), F32),
        ],
        in_specs=[VM, SM] + [VM] * 4 + [ANY] + [VM] * 4,
        out_specs=[VM] * 3,
        scratch_shapes=[
            pltpu.VMEM((NJ + 4, 8, NK), F32),
            pltpu.VMEM((2 * LN, NK), BF16),
            pltpu.VMEM((2, LN, HALF), F32),
            pltpu.VMEM((2, LN, NK), F32),
            pltpu.SemaphoreType.DMA(()),
        ],
        compiler_params=params(4),
        name="border",
    )(coef, edge, part, plane, lo, hi, faces, ghost_w, edge_w, face_w, flip_w)


def finish_kernel(
    coef, part, plane, lo, hi, faces, ghost_w, face_w, flip_w,
    out, window, stack, held, sems, near, sem,
):
    brought = pltpu.make_async_copy(faces, near, sem)
    brought.start()
    fill_window(window, lo, hi, plane)
    brought.wait()

    def copies(step, slot):
        rows = pl.ds(step * BLOCK, BLOCK)
        return [
            pltpu.make_async_copy(held.at[slot, h], out.at[:, rows, lanes(h)], sems.at[slot, h])
            for h in range(2)
        ]

    def keep(slot, n, j, change):
        for h in range(2):
            half = held.at[slot, h].reshape(LN * BLOCK, HALF)
            half[pl.ds(n, LN, stride=BLOCK), :] = part[j, h] + change[:, h * HALF : (h + 1) * HALF]

    first = turned_face(near.at[1], stack, face_w, flip_w)
    last = turned_face(near.at[0], stack, face_w, flip_w)

    def pair(step, carry):
        for slot in range(2):
            at = 2 * step + slot

            @pl.when(step > 0)
            def _():
                for copy in copies(at - 2, slot):
                    copy.wait()

            for n in range(BLOCK):
                j = at * BLOCK + n
                change = mul(ghost_w[...], blend_ghosts(coef, window, j))
                if n == 0 and slot == 0:
                    change = change + first * jnp.where(step == 0, 1.0, 0.0)
                if n == BLOCK - 1 and slot == 1:
                    change = change + last * jnp.where(step == STEPS // 2 - 1, 1.0, 0.0)
                keep(slot, n, j, change)
            for copy in copies(at, slot):
                copy.start()
        return carry

    lax.fori_loop(0, STEPS // 2, pair, 0)
    for step in range(STEPS - 2, STEPS):
        for copy in copies(step, step % 2):
            copy.wait()


def finish(coef, part, plane, lo, hi, faces, ghost_w, face_w, flip_w):
    return pl.pallas_call(
        finish_kernel,
        out_shape=jax.ShapeDtypeStruct((LN, NJ, NK), F32),
        in_specs=[VM] * 5 + [ANY] + [VM] * 3,
        out_specs=ANY,
        scratch_shapes=[
            pltpu.VMEM((NJ + 4, 8, NK), F32),
            pltpu.VMEM((2 * LN, NK), BF16),
            pltpu.VMEM((2, 2, LN, BLOCK, HALF), F32),
            pltpu.SemaphoreType.DMA((2, 2)),
            pltpu.VMEM((2, LN, NK), F32),
            pltpu.SemaphoreType.DMA(()),
        ],
        compiler_params=params(8),
        name="finish",
    )(coef, part, plane, lo, hi, faces, ghost_w, face_w, flip_w)


def exchange(plane, blocks):
    def across(step):
        return [
            (r * blocks + b, (1 - r) * blocks + (b + step) % blocks)
            for r in range(2)
            for b in range(blocks)
        ]

    axes = ("row", "blk")
    other = lax.ppermute(plane, "row", [(0, 1), (1, 0)])
    lo = lax.ppermute(plane[NJ - 2 :], axes, across(1))
    hi = lax.ppermute(plane[:2], axes, across(-1))
    return other, lo, hi


def beside(faces, bit, blocks, work, *operands):
    def branch(k):
        def run(faces, *operands):
            received = lax.ppermute(faces, "blk", [(b, b ^ (1 << k)) for b in range(blocks)])
            return received, work(*operands)

        return run

    return lax.switch(bit, [branch(k) for k in range(3)], faces, *operands)


def body(flow_state, forcing, stiffness, advection, line_inverse, margin_rows, margin_weights, partner_bit, turn_code):
    blocks = lax.axis_size("blk")
    row = lax.axis_index("row")
    bit = partner_bit[0, 0]
    state = in_hbm(flow_state.reshape(LN, NJ, NK))
    source = in_hbm(forcing.reshape(LN, NJ, NK))
    diagonal = in_hbm(stiffness.reshape(NI, NJ, NK))
    edge = jnp.where(row == 0, NI - 1, 0).reshape(1)
    faces, plane = begin(edge, state)
    comm = exchange(plane, blocks)
    flags = jnp.stack([row, turn_code[0, 0]])
    jac = jnp.pad(advection[0, 0], ((0, 2), (0, 2)))
    sweep_w, ghost_w, edge_w, face_w, flip_w, coef = prepare(
        flags, line_inverse[0, 0], jac, margin_rows[0, 0].T, margin_weights[0, 0].T
    )
    received, part = beside(faces, bit, blocks, interior, state, source, diagonal, sweep_w)
    for sweep in range(SWEEPS - 1):
        ghosts, faces, plane = border(
            coef, edge, part, *comm, received, ghost_w, edge_w, face_w, flip_w
        )
        comm = exchange(plane, blocks)
        received, part = beside(
            faces, bit, blocks, advance, part, ghosts, faces, source, diagonal, sweep_w, ghost_w
        )
    out = finish(coef, part, *comm, received, ghost_w, face_w, flip_w)
    return out.reshape(flow_state.shape)


def solution(mesh):
    return jax.shard_map(
        body,
        mesh=mesh,
        in_specs=(P("row", "blk"),) * 9,
        out_specs=P("row", "blk"),
        check_vma=False,
    )
```
